256 devices in a mesh: seq: 32 (over x, z), head: 8 (over y, core).
Axes of the slice: x: 4, y: 4, z: 8, core: 2. Of those that a mesh axis runs over, the one named last changes fastest.
Arguments:
- query_projection: bfloat16 [8192, 4096], P(('seq', 'head')), may hold values from -6 to 6
- key_projection: bfloat16 [8192, 1024], P(('seq', 'head')), may hold values from -6 to 6
- value_projection: bfloat16 [8192, 1024], P(('seq', 'head')), may hold values from -6 to 6
- output_gradient: bfloat16 [8192, 4096], P(('seq', 'head')), may hold values from -6 to 6
- partners: int32 [64, 6], P('seq'), may hold values from -1 to 62, as said below
Outputs:
- attention: bfloat16 [8192, 4096], P('seq', 'head')
- grad_query: bfloat16 [8192, 4096], P('seq', 'head')
- key_gradient: bfloat16 [8192, 1024], P('seq', 'head')
- value_gradient: bfloat16 [8192, 1024], P('seq', 'head')
The draws below stay inside these ranges and needn't reach their ends.
Inputs may be any that keep to these rules, and one draw needn't show every extreme that they name: For l < 1, partners[b, l] is -1 if b < 2**l, else a block at a distance of 2**l to 2**(l+1) - 1 blocks before b (not before block 0). For l = 1 + j, with g = b // 2 - 2**j, it is -1 if g < 0, else one of the blocks g * 2 to g * 2 + 1.
All inputs are finite; a program needn't handle non-finite values.
Results may differ from the reference program's by a relative error of at most 0.012.
Values may be sent and summed in bfloat16 or wider, within the bound.
No kernel may reach another device: no remote copies, remote signals or barrier semaphores. Data moves between devices by JAX's collectives and lax.ppermute only.
A program may use at most 64 MiB of HBM per device.

```python
import math
import jax
import jax.numpy as jnp
from jax import lax

QUERY_HEADS = 32
KEY_VALUE_HEADS = 8
HEAD_SIZE = 128
BLOCK_TOKENS = 128
SEQUENCE_TOKENS = 8192
BLK_DEV = 2
NBLK = 64
NEAR = 1
FAR = 5
LEVELS = 6


def drawn_fields(key):
    base_key = jax.random.fold_in(key, 11)
    key_query = jax.random.fold_in(base_key, 1)
    key_random_keys = jax.random.fold_in(base_key, 2)
    query_field = jnp.clip(jax.random.normal(key_query, (SEQUENCE_TOKENS, QUERY_HEADS * HEAD_SIZE), jnp.float32), -4.0, 4.0)
    key_table = jnp.clip(jax.random.normal(key_random_keys, (SEQUENCE_TOKENS, KEY_VALUE_HEADS * HEAD_SIZE), jnp.float32), -4.0, 4.0)
    return (query_field, key_table)


def draw_query_projection(key, part):
    return drawn_fields(key)[0].astype(jnp.bfloat16)


def draw_key_projection(key, part):
    return drawn_fields(key)[1].astype(jnp.bfloat16)


def draw_partners(key, part):
    block_indices = jnp.arange(NBLK, dtype=jnp.int32)
    columns = []
    for degree in range(NEAR):
        sub_key = jax.random.fold_in(key, degree)
        span = 2 ** degree
        highest = block_indices - span
        lowest = jnp.maximum(block_indices - 2 * span + 1, 0)
        spread = jnp.maximum(highest - lowest + 1, 1)
        offset = jax.random.randint(sub_key, (NBLK,), 0, span) % spread
        columns.append(jnp.where(highest >= 0, highest - offset, -1))
    for degree in range(FAR):
        sub_key = jax.random.fold_in(key, 100 + degree)
        group_id = block_indices // BLK_DEV - 2 ** degree
        offset = jax.random.randint(sub_key, (NBLK,), 0, BLK_DEV)
        columns.append(jnp.where(group_id >= 0, group_id * BLK_DEV + offset, -1))
    return jnp.stack(columns, axis=1).astype(jnp.int32)


def block_scale(key, extent, cuts, least, top_value):
    def one(dim, blocks):
        heights = jax.random.uniform(jax.random.fold_in(jax.random.fold_in(key, 6), dim), (blocks,), jnp.float32, least / len(cuts), top_value / len(cuts))
        return jnp.repeat(jnp.exp(heights), extent[dim] // blocks).reshape((-1,) + (1,) * (len(extent) - dim - 1))

    gain = one(*cuts[0])
    for cut in cuts[1:]:
        gain = gain * one(*cut)
    return gain


def centred(stream_key, extent, width, reach, split=(), kind=jnp.bfloat16):
    drawn = jax.random.normal(stream_key, extent, jnp.float32) * width
    if len(split) > 0:
        drawn = block_scale(stream_key, extent, split, -0.22, 0.18) * drawn
    return jnp.clip(drawn, min=-reach, max=reach).astype(kind)


def setup_inputs(seed: int = 0) -> dict:
    key_of = jax.random.split(jax.random.key(seed), 6)
    query_projection = draw_query_projection(jax.random.fold_in(key_of[5], 71), 0)
    key_projection = draw_key_projection(jax.random.fold_in(key_of[5], 71), 0)
    value_projection = centred(key_of[2], (SEQUENCE_TOKENS, KEY_VALUE_HEADS * HEAD_SIZE), 1.0, 6.0, ((0, 256),))
    output_gradient = centred(key_of[3], (SEQUENCE_TOKENS, QUERY_HEADS * HEAD_SIZE), 1.0, 6.0, ((0, 256),))
    partners = draw_partners(jax.random.fold_in(key_of[5], 71), 0)
    return {"query_projection": query_projection, "key_projection": key_projection, "value_projection": value_projection, "output_gradient": output_gradient, "partners": partners}


masked_score = -1e+30

def reference(query_projection, key_projection, value_projection, output_gradient, partners):
    token_count_all = query_projection.shape[0]
    block_count_all = token_count_all // BLOCK_TOKENS
    heads_per_group = QUERY_HEADS // KEY_VALUE_HEADS
    slot_count_all = 1 + LEVELS
    key_number = slot_count_all * BLOCK_TOKENS
    scaling = 1.0 / math.sqrt(HEAD_SIZE)
    highest = lax.Precision.HIGHEST
    query_block_set = query_projection.reshape(block_count_all, BLOCK_TOKENS, KEY_VALUE_HEADS, heads_per_group, HEAD_SIZE)
    output_grad_blocks = output_gradient.reshape(block_count_all, BLOCK_TOKENS, KEY_VALUE_HEADS, heads_per_group, HEAD_SIZE)
    key_blocks = key_projection.reshape(block_count_all, BLOCK_TOKENS, KEY_VALUE_HEADS, HEAD_SIZE)
    value_blocks = value_projection.reshape(block_count_all, BLOCK_TOKENS, KEY_VALUE_HEADS, HEAD_SIZE)
    row_ids = jnp.arange(BLOCK_TOKENS)[:, None]
    columns = jnp.arange(key_number)[None, :]
    slot_of = columns // BLOCK_TOKENS
    causal = (slot_of == 0) & (columns <= row_ids)

    def step(accum, inputs):
        key_accumulator, value_accumulator = accum
        block_id, partner_row = inputs
        is_valid = partner_row >= 0
        block_indices = jnp.concatenate([block_id[None], jnp.maximum(partner_row, 0)]).astype(jnp.int32)
        key_row_set = key_blocks[block_indices].reshape(key_number, KEY_VALUE_HEADS, HEAD_SIZE).astype(jnp.float32)
        value_row_set = value_blocks[block_indices].reshape(key_number, KEY_VALUE_HEADS, HEAD_SIZE).astype(jnp.float32)
        query_f = query_block_set[block_id].astype(jnp.float32)
        dout_f = output_grad_blocks[block_id].astype(jnp.float32)
        slot_valid = jnp.concatenate([jnp.ones((1,), bool), is_valid])
        allowed = causal | (slot_of > 0) & slot_valid[slot_of[0]][None, :]
        scores = scaling * jnp.einsum('tgzd,kgd->gztk', query_f, key_row_set, precision=highest)
        scores = jnp.where(allowed, scores, masked_score)
        row_max = lax.optimization_barrier(jnp.max(scores, axis=-1, keepdims=True))
        exp_scores = jnp.exp(scores - row_max)
        weights = exp_scores / lax.optimization_barrier(jnp.sum(exp_scores, axis=-1, keepdims=True))
        weights_reduced = lax.optimization_barrier(weights.astype(jnp.bfloat16)).astype(jnp.float32)
        attn = jnp.einsum('gztk,kgd->tgzd', weights_reduced, value_row_set, precision=highest)
        row_dot = jnp.transpose(lax.optimization_barrier(jnp.sum(dout_f * attn, axis=-1)), (1, 2, 0))[..., None]
        dweights = jnp.einsum('tgzd,kgd->gztk', dout_f, value_row_set, precision=highest)
        score_gradient = lax.optimization_barrier((weights * (dweights - row_dot)).astype(jnp.bfloat16)).astype(jnp.float32)
        grad_q = scaling * jnp.einsum('gztk,kgd->tgzd', score_gradient, key_row_set, precision=highest)
        key_portion = scaling * jnp.einsum('gztk,tgzd->kgd', score_gradient, query_f, precision=highest)
        value_portion = jnp.einsum('gztk,tgzd->kgd', weights_reduced, dout_f, precision=highest)
        slot_weighting = slot_valid.astype(jnp.float32)[:, None, None, None]
        key_accumulator = key_accumulator.at[block_indices].add(key_portion.reshape(slot_count_all, BLOCK_TOKENS, KEY_VALUE_HEADS, HEAD_SIZE) * slot_weighting)
        value_accumulator = value_accumulator.at[block_indices].add(value_portion.reshape(slot_count_all, BLOCK_TOKENS, KEY_VALUE_HEADS, HEAD_SIZE) * slot_weighting)
        return ((key_accumulator, value_accumulator), (attn.astype(jnp.bfloat16), grad_q.astype(jnp.bfloat16)))
    zero_filled = jnp.zeros((block_count_all, BLOCK_TOKENS, KEY_VALUE_HEADS, HEAD_SIZE), jnp.float32)
    (key_accumulator, value_accumulator), (attn_all, grad_all) = lax.scan(step, (zero_filled, zero_filled), (jnp.arange(block_count_all, dtype=jnp.int32), partners))
    attention = attn_all.reshape(token_count_all, QUERY_HEADS * HEAD_SIZE)
    grad_query = grad_all.reshape(token_count_all, QUERY_HEADS * HEAD_SIZE)
    key_gradient = key_accumulator.reshape(token_count_all, KEY_VALUE_HEADS * HEAD_SIZE).astype(jnp.bfloat16)
    value_gradient = value_accumulator.reshape(token_count_all, KEY_VALUE_HEADS * HEAD_SIZE).astype(jnp.bfloat16)
    return (attention, grad_query, key_gradient, value_gradient)
```

```python
import functools
import math

import jax
import jax.numpy as jnp
from jax import lax
from jax.experimental import pallas as pl
from jax.experimental.pallas import tpu as pltpu
from jax.sharding import PartitionSpec as P

HEAD_SIZE = 128
BLOCK_TOKENS = 128
MASKED = -1e30
SCALING = 1.0 / math.sqrt(HEAD_SIZE)
VMEM = pl.BlockSpec(memory_space=pltpu.VMEM)
SMEM = pl.BlockSpec(memory_space=pltpu.SMEM)


def ring(value, axis, steps):
    count = lax.axis_size(axis)
    return lax.ppermute(value, axis, [(s, (s + steps) % count) for s in range(count)])


def pack_kernel(first_ref, second_ref, out_ref):
    heads, _, both = out_ref.shape
    width = both // 2
    for head in range(heads):
        columns = slice(head * width, (head + 1) * width)
        out_ref[head, :, :width] = first_ref[:, columns]
        out_ref[head, :, width:] = second_ref[:, columns]


def pack(first, second, heads):
    tokens, columns = first.shape
    return pl.pallas_call(
        pack_kernel,
        out_shape=jax.ShapeDtypeStruct((heads, tokens, 2 * columns // heads), first.dtype),
        in_specs=[VMEM, VMEM],
        out_specs=VMEM,
        compiler_params=pltpu.CompilerParams(vmem_limit_bytes=8 << 20),
    )(first, second)


def dot(a, b, contract):
    return lax.dot_general(a, b, ((contract[:1], contract[1:]), ((), ())), preferred_element_type=jnp.float32)


def main_kernel(far_count, q_heads, partners_ref, qd_ref, kv_ref, *refs):
    far_refs = refs[:far_count]
    own_ref, probs_ref, dscores_ref, cat_ref = refs[far_count : far_count + 4]
    part_refs = refs[far_count + 4 : 2 * far_count + 4]
    (sums_ref,) = refs[2 * far_count + 4 :]
    blocks = kv_ref.shape[0] // BLOCK_TOKENS
    slots = 2 + far_count
    size = BLOCK_TOKENS
    q_columns = q_heads * HEAD_SIZE
    pair = 2

    for b in range(blocks):
        rows = slice(b * size, (b + 1) * size)
        near = kv_ref[(b - 1) * size : b * size, :] if b else far_refs[0][(blocks - 1) * size :, :]
        cat_ref[b, :size, :] = kv_ref[rows, :]
        cat_ref[b, size : 2 * size, :] = near
        for j in range(far_count):
            pick = pl.multiple_of((partners_ref[b, 1 + j] & (blocks - 1)) * size, size)
            cat_ref[b, (2 + j) * size : (3 + j) * size, :] = far_refs[j][pl.ds(pick, size), :]

    causal = lax.broadcasted_iota(jnp.int32, (size, size), 0) <= lax.broadcasted_iota(jnp.int32, (size, size), 1)
    causal = jnp.concatenate([causal] * pair, axis=1)
    for b in range(blocks):
        rows = slice(b * size, (b + 1) * size)
        keys = cat_ref[b, :, :HEAD_SIZE]
        values = cat_ref[b, :, HEAD_SIZE:]
        bias = [jnp.where(partners_ref[b, l] >= 0, 0.0, MASKED).astype(jnp.float32) for l in range(1 + far_count)]
        queries, cotangents = [], []
        for h in range(q_heads):
            queries.append(qd_ref[rows, h * HEAD_SIZE : (h + 1) * HEAD_SIZE])
            cotangents.append(qd_ref[rows, q_columns + h * HEAD_SIZE : q_columns + (h + 1) * HEAD_SIZE])
        for c in range(q_heads // pair):
            columns = slice(c * pair * size, (c + 1) * pair * size)
            query = jnp.concatenate(queries[c * pair : (c + 1) * pair], axis=0)
            cotangent = jnp.concatenate(cotangents[c * pair : (c + 1) * pair], axis=0)
            raw = dot(keys, query, (1, 1))
            scores = [jnp.where(causal, raw[:size], MASKED)]
            scores += [raw[(1 + l) * size : (2 + l) * size] + bias[l] for l in range(1 + far_count)]
            top = functools.reduce(jnp.maximum, scores)
            top = jnp.max(top, axis=0, keepdims=True)
            weights = [jnp.exp((s - top) * SCALING) for s in scores]
            total = jnp.sum(functools.reduce(jnp.add, weights), axis=0, keepdims=True)
            inverse = 1.0 / total
            dprobs = dot(values, cotangent, (1, 1))
            row_dot = jnp.zeros((size, pair * size), jnp.float32)
            for i in range(slots):
                weights[i] = weights[i] * inverse
                low = weights[i].astype(jnp.bfloat16)
                probs_ref[b, i * size : (i + 1) * size, columns] = low
                row_dot = row_dot + low.astype(jnp.float32) * dprobs[i * size : (i + 1) * size]
            row_dot = jnp.sum(row_dot, axis=0, keepdims=True)
            for i in range(slots):
                change = weights[i] * (dprobs[i * size : (i + 1) * size] - row_dot)
                dscores_ref[b, i * size : (i + 1) * size, columns] = change.astype(jnp.bfloat16)
        sums_ref[b, :, :HEAD_SIZE] = SCALING * dot(dscores_ref[b], jnp.concatenate(queries, axis=0), (1, 0))
        sums_ref[b, :, HEAD_SIZE:] = dot(probs_ref[b], jnp.concatenate(cotangents, axis=0), (1, 0))

    for b in range(blocks):
        total = sums_ref[b, :size, :]
        if b + 1 < blocks:
            total = total + sums_ref[b + 1, size : 2 * size, :]
        own_ref[b * size : (b + 1) * size, :] = total
    for j in range(far_count):
        at = slice((2 + j) * size, (3 + j) * size)
        for target in range(blocks):
            total = None
            for b in range(blocks):
                chosen = (partners_ref[b, 1 + j] & (blocks - 1)) == target
                term = jnp.where(chosen, sums_ref[b, at, :], 0.0)
                total = term if total is None else total + term
            if j == 0 and target == blocks - 1:
                total = total + sums_ref[0, size : 2 * size, :]
            part_refs[j][target * size : (target + 1) * size, :] = total.astype(jnp.bfloat16)


def outputs_kernel(q_heads, probs_ref, dscores_ref, cat_ref, attention_ref, grad_query_ref):
    size = BLOCK_TOKENS
    for b in range(probs_ref.shape[0]):
        rows = slice(b * size, (b + 1) * size)
        attention = dot(cat_ref[b, :, HEAD_SIZE:], probs_ref[b], (0, 0))
        grad_query = SCALING * dot(cat_ref[b, :, :HEAD_SIZE], dscores_ref[b], (0, 0))
        for h in range(q_heads):
            columns = slice(h * HEAD_SIZE, (h + 1) * HEAD_SIZE)
            at = slice(h * size, (h + 1) * size)
            attention_ref[rows, columns] = attention[:, at].T.astype(jnp.bfloat16)
            grad_query_ref[rows, columns] = grad_query[:, at].T.astype(jnp.bfloat16)


def sum_kernel(own_ref, *refs):
    key_ref, value_ref = refs[-2:]
    total = own_ref[...]
    for ref in refs[:-2]:
        total = total + ref[...].astype(jnp.float32)
    key_ref[...] = total[:, :HEAD_SIZE].astype(jnp.bfloat16)
    value_ref[...] = total[:, HEAD_SIZE:].astype(jnp.bfloat16)


def shards(query_projection, key_projection, value_projection, output_gradient, partners):
    heads = lax.axis_size("head")
    kv = lax.all_to_all(pack(key_projection, value_projection, heads), "head", 0, 0, tiled=True)
    qd = lax.all_to_all(pack(query_projection, output_gradient, heads), "head", 0, 0, tiled=True)
    kv = kv.reshape(-1, kv.shape[-1])
    qd = qd.reshape(-1, qd.shape[-1])
    tokens = kv.shape[0]
    blocks = tokens // BLOCK_TOKENS
    q_heads = qd.shape[1] // (2 * HEAD_SIZE)
    far_count = partners.shape[1] - 1
    fars = [ring(kv, "seq", 2**j) for j in range(far_count)]
    keys = (2 + far_count) * BLOCK_TOKENS
    big = (blocks, keys, q_heads * BLOCK_TOKENS)
    own, probs, dscores, cat, *parts = pl.pallas_call(
        functools.partial(main_kernel, far_count, q_heads),
        out_shape=[
            jax.ShapeDtypeStruct((tokens, 2 * HEAD_SIZE), jnp.float32),
            jax.ShapeDtypeStruct(big, jnp.bfloat16),
            jax.ShapeDtypeStruct(big, jnp.bfloat16),
            jax.ShapeDtypeStruct((blocks, keys, 2 * HEAD_SIZE), jnp.bfloat16),
        ]
        + [jax.ShapeDtypeStruct((tokens, 2 * HEAD_SIZE), jnp.bfloat16)] * far_count,
        in_specs=[SMEM] + [VMEM] * (2 + far_count),
        out_specs=[VMEM] * (4 + far_count),
        scratch_shapes=[pltpu.VMEM((blocks, keys, 2 * HEAD_SIZE), jnp.float32)],
        compiler_params=pltpu.CompilerParams(vmem_limit_bytes=32 << 20),
    )(partners, qd, kv, *fars)
    received = [ring(part, "seq", -(2**j)) for j, part in enumerate(parts)]
    attention, grad_query = pl.pallas_call(
        functools.partial(outputs_kernel, q_heads),
        out_shape=[jax.ShapeDtypeStruct((tokens, q_heads * HEAD_SIZE), jnp.bfloat16)] * 2,
        in_specs=[VMEM] * 3,
        out_specs=[VMEM] * 2,
        compiler_params=pltpu.CompilerParams(vmem_limit_bytes=32 << 20),
    )(probs, dscores, cat)
    key_gradient, value_gradient = pl.pallas_call(
        sum_kernel,
        out_shape=[jax.ShapeDtypeStruct((tokens, HEAD_SIZE), jnp.bfloat16)] * 2,
        in_specs=[VMEM] * (1 + far_count),
        out_specs=[VMEM] * 2,
        compiler_params=pltpu.CompilerParams(vmem_limit_bytes=8 << 20),
    )(own, *received)
    return (attention, grad_query, key_gradient, value_gradient)


def solution(mesh):
    placed = (
        P(("seq", "head"), None),
        P(("seq", "head"), None),
        P(("seq", "head"), None),
        P(("seq", "head"), None),
        P("seq", None),
    )
    return jax.shard_map(
        shards,
        mesh=mesh,
        in_specs=placed,
        out_specs=(P("seq", "head"), P("seq", "head"), P("seq", "head"), P("seq", "head")),
        check_vma=False,
    )
```

```python
import functools
import math

import jax
import jax.numpy as jnp
from jax import lax
from jax.experimental import pallas as pl
from jax.experimental.pallas import tpu as pltpu
from jax.sharding import PartitionSpec as P

HEAD_SIZE = 128
BLOCK_TOKENS = 128
MASKED = -1e30
SCALING = 1.0 / math.sqrt(HEAD_SIZE)
VMEM = pl.BlockSpec(memory_space=pltpu.VMEM)
SMEM = pl.BlockSpec(memory_space=pltpu.SMEM)
HBM = pl.BlockSpec(memory_space=pltpu.HBM)
EARLY = (2, 0)


def ring(value, axis, steps):
    count = lax.axis_size(axis)
    return lax.ppermute(value, axis, [(s, (s + steps) % count) for s in range(count)])


def pack_kernel(*refs):
    sources, packed, sems = refs[:4], refs[4:6], refs[6]
    heads = packed[0].shape[0]
    copies = []
    for i, source in enumerate(sources):
        target = packed[i // 2]
        width = source.shape[1] // heads
        for head in range(heads):
            copies.append(
                pltpu.make_async_copy(
                    source.at[:, pl.ds(head * width, width)],
                    target.at[head, :, pl.ds((i % 2) * width, width)],
                    sems.at[i, head],
                )
            )
    for copy in copies:
        copy.start()
    for copy in copies:
        copy.wait()


def pack(arrays, heads):
    def packed(array):
        return jax.ShapeDtypeStruct((heads, array.shape[0], 2 * array.shape[1] // heads), array.dtype)

    return pl.pallas_call(
        pack_kernel,
        out_shape=[packed(arrays[0]), packed(arrays[2])],
        in_specs=[HBM] * 4,
        out_specs=[VMEM] * 2,
        scratch_shapes=[pltpu.SemaphoreType.DMA((4, heads))],
        compiler_params=pltpu.CompilerParams(vmem_limit_bytes=60 << 20),
    )(*arrays)


def dot(a, b, contract):
    return lax.dot_general(a, b, ((contract[:1], contract[1:]), ((), ())), preferred_element_type=jnp.float32)


def fill(cat_ref, partners_ref, fars, kv_ref=None):
    blocks = cat_ref.shape[0]
    size = BLOCK_TOKENS
    for b in range(blocks):
        if kv_ref is not None:
            cat_ref[b, :size, :] = kv_ref[b * size : (b + 1) * size, :]
            if b:
                cat_ref[b, size : 2 * size, :] = kv_ref[(b - 1) * size : b * size, :]
        for j, far_ref in fars.items():
            if b == 0 and j == 0:
                cat_ref[b, size : 2 * size, :] = far_ref[(blocks - 1) * size :, :]
            pick = pl.multiple_of((partners_ref[b, 1 + j] & (blocks - 1)) * size, size)
            cat_ref[b, (2 + j) * size : (3 + j) * size, :] = far_ref[pl.ds(pick, size), :]


def early_kernel(partners_ref, kv_ref, *refs):
    fill(refs[-1], partners_ref, dict(zip(EARLY, refs[:-1], strict=True)), kv_ref)


def main_kernel(far_count, q_heads, late, partners_ref, qd_ref, listed_ref, *refs):
    far_refs, refs = refs[: len(late)], refs[len(late) :]
    own_ref, probs_ref, dscores_ref, cat_ref = refs[:4]
    part_refs = refs[4 : 4 + far_count]
    (sums_ref,) = refs[4 + far_count :]
    blocks = cat_ref.shape[0]
    slots = 2 + far_count
    size = BLOCK_TOKENS
    q_columns = q_heads * HEAD_SIZE
    pair = 2
    fill(cat_ref, partners_ref, dict(zip(late, far_refs, strict=True)))

    causal = lax.broadcasted_iota(jnp.int32, (size, size), 0) <= lax.broadcasted_iota(jnp.int32, (size, size), 1)
    causal = jnp.concatenate([causal] * pair, axis=1)
    for b in range(blocks):
        rows = slice(b * size, (b + 1) * size)
        keys = cat_ref[b, :, :HEAD_SIZE]
        values = cat_ref[b, :, HEAD_SIZE:]
        bias = [jnp.where(partners_ref[b, l] >= 0, 0.0, MASKED).astype(jnp.float32) for l in range(1 + far_count)]
        queries, cotangents = [], []
        for h in range(q_heads):
            queries.append(qd_ref[rows, h * HEAD_SIZE : (h + 1) * HEAD_SIZE])
            cotangents.append(qd_ref[rows, q_columns + h * HEAD_SIZE : q_columns + (h + 1) * HEAD_SIZE])
        for c in range(q_heads // pair):
            columns = slice(c * pair * size, (c + 1) * pair * size)
            query = jnp.concatenate(queries[c * pair : (c + 1) * pair], axis=0)
            cotangent = jnp.concatenate(cotangents[c * pair : (c + 1) * pair], axis=0)
            raw = dot(keys, query, (1, 1))
            scores = [jnp.where(causal, raw[:size], MASKED)]
            scores += [raw[(1 + l) * size : (2 + l) * size] + bias[l] for l in range(1 + far_count)]
            top = functools.reduce(jnp.maximum, scores)
            top = jnp.max(top, axis=0, keepdims=True)
            weights = [jnp.exp((s - top) * SCALING) for s in scores]
            total = jnp.sum(functools.reduce(jnp.add, weights), axis=0, keepdims=True)
            inverse = 1.0 / total
            dprobs = dot(values, cotangent, (1, 1))
            row_dot = jnp.zeros((size, pair * size), jnp.float32)
            for i in range(slots):
                weights[i] = weights[i] * inverse
                low = weights[i].astype(jnp.bfloat16)
                probs_ref[b, i * size : (i + 1) * size, columns] = low
                row_dot = row_dot + low.astype(jnp.float32) * dprobs[i * size : (i + 1) * size]
            row_dot = jnp.sum(row_dot, axis=0, keepdims=True)
            for i in range(slots):
                change = weights[i] * (dprobs[i * size : (i + 1) * size] - row_dot)
                dscores_ref[b, i * size : (i + 1) * size, columns] = change.astype(jnp.bfloat16)
        sums_ref[b, :, :HEAD_SIZE] = SCALING * dot(dscores_ref[b], jnp.concatenate(queries, axis=0), (1, 0))
        sums_ref[b, :, HEAD_SIZE:] = dot(probs_ref[b], jnp.concatenate(cotangents, axis=0), (1, 0))

    for b in range(blocks):
        total = sums_ref[b, :size, :]
        if b + 1 < blocks:
            total = total + sums_ref[b + 1, size : 2 * size, :]
        own_ref[b * size : (b + 1) * size, :] = total
    for j in range(far_count):
        at = slice((2 + j) * size, (3 + j) * size)
        for target in range(blocks):
            total = None
            for b in range(blocks):
                chosen = (partners_ref[b, 1 + j] & (blocks - 1)) == target
                term = jnp.where(chosen, sums_ref[b, at, :], 0.0)
                total = term if total is None else total + term
            if j == 0 and target == blocks - 1:
                total = total + sums_ref[0, size : 2 * size, :]
            part_refs[j][target * size : (target + 1) * size, :] = total.astype(jnp.bfloat16)


def outputs_kernel(q_heads, probs_ref, dscores_ref, cat_ref, attention_ref, grad_query_ref):
    size = BLOCK_TOKENS
    for b in range(probs_ref.shape[0]):
        rows = slice(b * size, (b + 1) * size)
        attention = dot(cat_ref[b, :, HEAD_SIZE:], probs_ref[b], (0, 0))
        grad_query = SCALING * dot(cat_ref[b, :, :HEAD_SIZE], dscores_ref[b], (0, 0))
        for h in range(q_heads):
            columns = slice(h * HEAD_SIZE, (h + 1) * HEAD_SIZE)
            at = slice(h * size, (h + 1) * size)
            attention_ref[rows, columns] = attention[:, at].T.astype(jnp.bfloat16)
            grad_query_ref[rows, columns] = grad_query[:, at].T.astype(jnp.bfloat16)


def sum_kernel(own_ref, *refs):
    key_ref, value_ref = refs[-2:]
    total = own_ref[...]
    for ref in refs[:-2]:
        total = total + ref[...].astype(jnp.float32)
    key_ref[...] = total[:, :HEAD_SIZE].astype(jnp.bfloat16)
    value_ref[...] = total[:, HEAD_SIZE:].astype(jnp.bfloat16)


def shards(query_projection, key_projection, value_projection, output_gradient, partners):
    heads = lax.axis_size("head")
    kv, qd = pack((key_projection, value_projection, query_projection, output_gradient), heads)
    kv = lax.all_to_all(kv, "head", 0, 0, tiled=True)
    qd = lax.all_to_all(qd, "head", 0, 0, tiled=True)
    kv = kv.reshape(-1, kv.shape[-1])
    qd = qd.reshape(-1, qd.shape[-1])
    tokens = kv.shape[0]
    blocks = tokens // BLOCK_TOKENS
    q_heads = qd.shape[1] // (2 * HEAD_SIZE)
    far_count = partners.shape[1] - 1
    fars = {j: ring(kv, "seq", 2**j) for j in range(far_count) if j != 1}
    fars[1] = ring(fars[0], "seq", 1)
    late = (1, 4, 3)
    keys = (2 + far_count) * BLOCK_TOKENS
    big = (blocks, keys, q_heads * BLOCK_TOKENS)
    cat_type = jax.ShapeDtypeStruct((blocks, keys, 2 * HEAD_SIZE), jnp.bfloat16)
    listed = pl.pallas_call(
        early_kernel,
        out_shape=cat_type,
        in_specs=[SMEM] + [VMEM] * (1 + len(EARLY)),
        out_specs=VMEM,
        cost_estimate=pl.CostEstimate(flops=10**10, transcendentals=0, bytes_accessed=0),
        compiler_params=pltpu.CompilerParams(vmem_limit_bytes=8 << 20),
    )(partners, kv, *[fars[j] for j in EARLY])
    own, probs, dscores, cat, *parts = pl.pallas_call(
        functools.partial(main_kernel, far_count, q_heads, late),
        out_shape=[
            jax.ShapeDtypeStruct((tokens, 2 * HEAD_SIZE), jnp.float32),
            jax.ShapeDtypeStruct(big, jnp.bfloat16),
            jax.ShapeDtypeStruct(big, jnp.bfloat16),
            cat_type,
        ]
        + [jax.ShapeDtypeStruct((tokens, 2 * HEAD_SIZE), jnp.bfloat16)] * far_count,
        in_specs=[SMEM] + [VMEM] * (2 + len(late)),
        out_specs=[VMEM] * (4 + far_count),
        input_output_aliases={2: 3},
        scratch_shapes=[pltpu.VMEM((blocks, keys, 2 * HEAD_SIZE), jnp.float32)],
        compiler_params=pltpu.CompilerParams(vmem_limit_bytes=32 << 20),
    )(partners, qd, listed, *[fars[j] for j in late])
    received = [ring(part, "seq", -(2**j)) for j, part in enumerate(parts)]
    attention, grad_query = pl.pallas_call(
        functools.partial(outputs_kernel, q_heads),
        out_shape=[jax.ShapeDtypeStruct((tokens, q_heads * HEAD_SIZE), jnp.bfloat16)] * 2,
        in_specs=[VMEM] * 3,
        out_specs=[VMEM] * 2,
        compiler_params=pltpu.CompilerParams(vmem_limit_bytes=32 << 20),
    )(probs, dscores, cat)
    key_gradient, value_gradient = pl.pallas_call(
        sum_kernel,
        out_shape=[jax.ShapeDtypeStruct((tokens, HEAD_SIZE), jnp.bfloat16)] * 2,
        in_specs=[VMEM] * (1 + far_count),
        out_specs=[VMEM] * 2,
        compiler_params=pltpu.CompilerParams(vmem_limit_bytes=8 << 20),
    )(own, *received)
    return (attention, grad_query, key_gradient, value_gradient)


def solution(mesh):
    placed = (
        P(("seq", "head"), None),
        P(("seq", "head"), None),
        P(("seq", "head"), None),
        P(("seq", "head"), None),
        P("seq", None),
    )
    return jax.shard_map(
        shards,
        mesh=mesh,
        in_specs=placed,
        out_specs=(P("seq", "head"), P("seq", "head"), P("seq", "head"), P("seq", "head")),
        check_vma=False,
    )
```

```python
import functools
import math

import jax
import jax.numpy as jnp
from jax import lax
from jax.experimental import pallas as pl
from jax.experimental.pallas import tpu as pltpu
from jax.sharding import PartitionSpec as P

HEAD_SIZE = 128
BLOCK_TOKENS = 128
MASKED = -1e30
SCALING = 1.0 / math.sqrt(HEAD_SIZE)
VMEM = pl.BlockSpec(memory_space=pltpu.VMEM)
SMEM = pl.BlockSpec(memory_space=pltpu.SMEM)
HBM = pl.BlockSpec(memory_space=pltpu.HBM)
EARLY = (2, 0)


def ring(value, axis, steps):
    count = lax.axis_size(axis)
    return lax.ppermute(value, axis, [(s, (s + steps) % count) for s in range(count)])


def line(value, axis, steps):
    count = lax.axis_size(axis)
    pairs = [(s, s + steps) for s in range(count) if 0 <= s + steps < count]
    return lax.ppermute(value, axis, pairs)


def pack_kernel(*refs):
    sources, packed, held = refs[:4], refs[4:6], refs[6:8]
    in_sems, out_sems = refs[8:]
    heads = packed[0].shape[0]

    def arrival(i, head):
        width = sources[i].shape[1] // heads
        return pltpu.make_async_copy(
            sources[i].at[:, pl.ds(head * width, width)],
            held[i // 2].at[head, :, pl.ds((i % 2) * width, width)],
            in_sems.at[i, head],
        )

    def departure(k, head):
        return pltpu.make_async_copy(held[k].at[head], packed[k].at[head], out_sems.at[k, head])

    for k in range(2):
        for head in range(heads):
            arrival(2 * k, head).start()
            arrival(2 * k + 1, head).start()
    for k in range(2):
        for head in range(heads):
            arrival(2 * k, head).wait()
            arrival(2 * k + 1, head).wait()
            departure(k, head).start()
    for k in range(2):
        for head in range(heads):
            departure(k, head).wait()


def pack(arrays, heads):
    shapes = [(heads, a.shape[0], 2 * a.shape[1] // heads) for a in (arrays[0], arrays[2])]
    dtype = arrays[0].dtype
    return pl.pallas_call(
        pack_kernel,
        out_shape=[jax.ShapeDtypeStruct(shape, dtype) for shape in shapes],
        in_specs=[HBM] * 4,
        out_specs=[HBM] * 2,
        scratch_shapes=[
            *[pltpu.VMEM(shape, dtype) for shape in shapes],
            pltpu.SemaphoreType.DMA((4, heads)),
            pltpu.SemaphoreType.DMA((2, heads)),
        ],
        compiler_params=pltpu.CompilerParams(vmem_limit_bytes=60 << 20),
    )(*arrays)


def dot(a, b, contract):
    return lax.dot_general(a, b, ((contract[:1], contract[1:]), ((), ())), preferred_element_type=jnp.float32)


def fill(cat_ref, partners_ref, fars, kv_ref=None):
    blocks = cat_ref.shape[0]
    size = BLOCK_TOKENS
    for b in range(blocks):
        if kv_ref is not None:
            cat_ref[b, :size, :] = kv_ref[b * size : (b + 1) * size, :]
            if b:
                cat_ref[b, size : 2 * size, :] = kv_ref[(b - 1) * size : b * size, :]
        for j, far_ref in fars.items():
            if b == 0 and j == 0:
                cat_ref[b, size : 2 * size, :] = far_ref[(blocks - 1) * size :, :]
            pick = pl.multiple_of((partners_ref[b, 1 + j] & (blocks - 1)) * size, size)
            cat_ref[b, (2 + j) * size : (3 + j) * size, :] = far_ref[pl.ds(pick, size), :]


def early_kernel(partners_ref, kv_ref, *refs):
    fill(refs[-1], partners_ref, dict(zip(EARLY, refs[:-1], strict=True)), kv_ref)


def stack(qd_ref, b, first, heads):
    rows = slice(b * BLOCK_TOKENS, (b + 1) * BLOCK_TOKENS)
    columns = [slice((first + h) * HEAD_SIZE, (first + h + 1) * HEAD_SIZE) for h in range(heads)]
    return jnp.concatenate([qd_ref[rows, c] for c in columns], axis=0)


def gradients(probs_ref, dscores_ref, qd_ref, sums_ref, q_heads, b, low, high):
    rows = slice(low * BLOCK_TOKENS, high * BLOCK_TOKENS)
    query = stack(qd_ref, b, 0, q_heads)
    cotangent = stack(qd_ref, b, q_heads, q_heads)
    sums_ref[b, rows, :HEAD_SIZE] = SCALING * dot(dscores_ref[b, rows, :], query, (1, 0))
    sums_ref[b, rows, HEAD_SIZE:] = dot(probs_ref[b, rows, :], cotangent, (1, 0))


def main_kernel(far_count, q_heads, late, partners_ref, qd_ref, listed_ref, *refs):
    far_refs, refs = refs[: len(late)], refs[len(late) :]
    probs_ref, dscores_ref, cat_ref = refs[:3]
    part_refs = refs[3 : 3 + far_count]
    (sums_ref,) = refs[3 + far_count :]
    blocks = cat_ref.shape[0]
    slots = 2 + far_count
    size = BLOCK_TOKENS
    q_columns = q_heads * HEAD_SIZE
    pair = 2
    fill(cat_ref, partners_ref, dict(zip(late, far_refs, strict=True)))

    causal = lax.broadcasted_iota(jnp.int32, (size, size), 0) <= lax.broadcasted_iota(jnp.int32, (size, size), 1)
    causal = jnp.concatenate([causal] * pair, axis=1)
    for b in range(blocks):
        rows = slice(b * size, (b + 1) * size)
        keys = cat_ref[b, :, :HEAD_SIZE]
        values = cat_ref[b, :, HEAD_SIZE:]
        bias = [jnp.where(partners_ref[b, l] >= 0, 0.0, MASKED).astype(jnp.float32) for l in range(1 + far_count)]
        queries, cotangents = [], []
        for h in range(q_heads):
            queries.append(qd_ref[rows, h * HEAD_SIZE : (h + 1) * HEAD_SIZE])
            cotangents.append(qd_ref[rows, q_columns + h * HEAD_SIZE : q_columns + (h + 1) * HEAD_SIZE])
        for c in range(q_heads // pair):
            columns = slice(c * pair * size, (c + 1) * pair * size)
            query = jnp.concatenate(queries[c * pair : (c + 1) * pair], axis=0)
            cotangent = jnp.concatenate(cotangents[c * pair : (c + 1) * pair], axis=0)
            raw = dot(keys, query, (1, 1))
            scores = [jnp.where(causal, raw[:size], MASKED)]
            scores += [raw[(1 + l) * size : (2 + l) * size] + bias[l] for l in range(1 + far_count)]
            top = functools.reduce(jnp.maximum, scores)
            top = jnp.max(top, axis=0, keepdims=True)
            weights = [jnp.exp2((s - top) * (SCALING * math.log2(math.e))) for s in scores]
            total = jnp.sum(functools.reduce(jnp.add, weights), axis=0, keepdims=True)
            inverse = 1.0 / total
            dprobs = dot(values, cotangent, (1, 1))
            row_dot = jnp.zeros((size, pair * size), jnp.float32)
            for i in range(slots):
                weights[i] = weights[i] * inverse
                low = weights[i].astype(jnp.bfloat16)
                probs_ref[b, i * size : (i + 1) * size, columns] = low
                row_dot = row_dot + low.astype(jnp.float32) * dprobs[i * size : (i + 1) * size]
            row_dot = jnp.sum(row_dot, axis=0, keepdims=True)
            for i in range(slots):
                change = weights[i] * (dprobs[i * size : (i + 1) * size] - row_dot)
                dscores_ref[b, i * size : (i + 1) * size, columns] = change.astype(jnp.bfloat16)
        gradients(probs_ref, dscores_ref, qd_ref, sums_ref, q_heads, b, 2 if b else 1, slots)
    for j in range(far_count):
        at = slice((2 + j) * size, (3 + j) * size)
        for target in range(blocks):
            total = None
            for b in range(blocks):
                chosen = (partners_ref[b, 1 + j] & (blocks - 1)) == target
                term = jnp.where(chosen, sums_ref[b, at, :], 0.0)
                total = term if total is None else total + term
            if j == 0 and target == blocks - 1:
                total = total + sums_ref[0, size : 2 * size, :]
            part_refs[j][target * size : (target + 1) * size, :] = total.astype(jnp.bfloat16)


def outputs_kernel(q_heads, qd_ref, probs_ref, dscores_ref, cat_ref, attention_ref, grad_query_ref, own_ref, sums_ref):
    size = BLOCK_TOKENS
    blocks = probs_ref.shape[0]
    for b in range(blocks):
        rows = slice(b * size, (b + 1) * size)
        attention = dot(cat_ref[b, :, HEAD_SIZE:], probs_ref[b], (0, 0))
        grad_query = SCALING * dot(cat_ref[b, :, :HEAD_SIZE], dscores_ref[b], (0, 0))
        for h in range(q_heads):
            columns = slice(h * HEAD_SIZE, (h + 1) * HEAD_SIZE)
            at = slice(h * size, (h + 1) * size)
            attention_ref[rows, columns] = attention[:, at].T.astype(jnp.bfloat16)
            grad_query_ref[rows, columns] = grad_query[:, at].T.astype(jnp.bfloat16)
        gradients(probs_ref, dscores_ref, qd_ref, sums_ref, q_heads, b, 0, 2 if b else 1)
    for b in range(blocks):
        total = sums_ref[b, :size, :]
        if b + 1 < blocks:
            total = total + sums_ref[b + 1, size : 2 * size, :]
        own_ref[b * size : (b + 1) * size, :] = total


def sum_kernel(own_ref, *refs):
    key_ref, value_ref = refs[-2:]
    total = own_ref[...]
    for ref in refs[:-2]:
        total = total + ref[...].astype(jnp.float32)
    key_ref[...] = total[:, :HEAD_SIZE].astype(jnp.bfloat16)
    value_ref[...] = total[:, HEAD_SIZE:].astype(jnp.bfloat16)


def shards(query_projection, key_projection, value_projection, output_gradient, partners):
    heads = lax.axis_size("head")
    kv, qd = pack((key_projection, value_projection, query_projection, output_gradient), heads)
    kv = lax.all_to_all(kv, "head", 0, 0, tiled=True)
    qd = lax.all_to_all(qd, "head", 0, 0, tiled=True)
    kv = kv.reshape(-1, kv.shape[-1])
    qd = qd.reshape(-1, qd.shape[-1])
    tokens = kv.shape[0]
    blocks = tokens // BLOCK_TOKENS
    q_heads = qd.shape[1] // (2 * HEAD_SIZE)
    far_count = partners.shape[1] - 1
    fars = {j: (line if j in (4,) else ring)(kv, "seq", 2**j) for j in range(far_count) if j != 1}
    fars[1] = ring(fars[0], "seq", 1)
    late = (1, 4, 3)
    keys = (2 + far_count) * BLOCK_TOKENS
    big = (blocks, keys, q_heads * BLOCK_TOKENS)
    cat_type = jax.ShapeDtypeStruct((blocks, keys, 2 * HEAD_SIZE), jnp.bfloat16)
    listed = pl.pallas_call(
        early_kernel,
        out_shape=cat_type,
        in_specs=[SMEM] + [VMEM] * (1 + len(EARLY)),
        out_specs=VMEM,
        cost_estimate=pl.CostEstimate(flops=10**10, transcendentals=0, bytes_accessed=0),
        compiler_params=pltpu.CompilerParams(vmem_limit_bytes=8 << 20),
    )(partners, kv, *[fars[j] for j in EARLY])
    probs, dscores, cat, *parts = pl.pallas_call(
        functools.partial(main_kernel, far_count, q_heads, late),
        out_shape=[
            jax.ShapeDtypeStruct(big, jnp.bfloat16),
            jax.ShapeDtypeStruct(big, jnp.bfloat16),
            cat_type,
        ]
        + [jax.ShapeDtypeStruct((tokens, 2 * HEAD_SIZE), jnp.bfloat16)] * far_count,
        in_specs=[SMEM] + [VMEM] * (2 + len(late)),
        out_specs=[VMEM] * (3 + far_count),
        input_output_aliases={2: 2},
        scratch_shapes=[pltpu.VMEM((blocks, keys, 2 * HEAD_SIZE), jnp.float32)],
        compiler_params=pltpu.CompilerParams(vmem_limit_bytes=32 << 20),
    )(partners, qd, listed, *[fars[j] for j in late])
    received = [(line if j in (4,) else ring)(part, "seq", -(2**j)) for j, part in enumerate(parts)]
    attention, grad_query, own = pl.pallas_call(
        functools.partial(outputs_kernel, q_heads),
        out_shape=[jax.ShapeDtypeStruct((tokens, q_heads * HEAD_SIZE), jnp.bfloat16)] * 2
        + [jax.ShapeDtypeStruct((tokens, 2 * HEAD_SIZE), jnp.float32)],
        in_specs=[VMEM] * 4,
        out_specs=[VMEM] * 3,
        scratch_shapes=[pltpu.VMEM((blocks, 2 * BLOCK_TOKENS, 2 * HEAD_SIZE), jnp.float32)],
        compiler_params=pltpu.CompilerParams(vmem_limit_bytes=32 << 20),
    )(qd, probs, dscores, cat)
    key_gradient, value_gradient = pl.pallas_call(
        sum_kernel,
        out_shape=[jax.ShapeDtypeStruct((tokens, HEAD_SIZE), jnp.bfloat16)] * 2,
        in_specs=[VMEM] * (1 + far_count),
        out_specs=[VMEM] * 2,
        compiler_params=pltpu.CompilerParams(vmem_limit_bytes=8 << 20),
    )(own, *received)
    return (attention, grad_query, key_gradient, value_gradient)


def solution(mesh):
    placed = (
        P(("seq", "head"), None),
        P(("seq", "head"), None),
        P(("seq", "head"), None),
        P(("seq", "head"), None),
        P("seq", None),
    )
    return jax.shard_map(
        shards,
        mesh=mesh,
        in_specs=placed,
        out_specs=(P("seq", "head"), P("seq", "head"), P("seq", "head"), P("seq", "head")),
        check_vma=False,
    )
```

```python
import functools
import math

import jax
import jax.numpy as jnp
from jax import lax
from jax.experimental import pallas as pl
from jax.experimental.pallas import tpu as pltpu
from jax.sharding import PartitionSpec as P

HEAD_SIZE = 128
BLOCK_TOKENS = 128
MASKED = -1e30
SCALING = 1.0 / math.sqrt(HEAD_SIZE)
VMEM = pl.BlockSpec(memory_space=pltpu.VMEM)
SMEM = pl.BlockSpec(memory_space=pltpu.SMEM)
HBM = pl.BlockSpec(memory_space=pltpu.HBM)
EARLY = (2, 0)


def ring(value, axis, steps):
    count = lax.axis_size(axis)
    return lax.ppermute(value, axis, [(s, (s + steps) % count) for s in range(count)])


def line(value, axis, steps):
    count = lax.axis_size(axis)
    pairs = [(s, s + steps) for s in range(count) if 0 <= s + steps < count]
    return lax.ppermute(value, axis, pairs)


def pack_kernel(*refs):
    sources, packed, held = refs[:4], refs[4:6], refs[6:8]
    in_sems, out_sems = refs[8:]
    heads = packed[0].shape[0]

    def arrival(i, head):
        width = sources[i].shape[1] // heads
        return pltpu.make_async_copy(
            sources[i].at[:, pl.ds(head * width, width)],
            held[i // 2].at[head, :, pl.ds((i % 2) * width, width)],
            in_sems.at[i, head],
        )

    def departure(k, head):
        return pltpu.make_async_copy(held[k].at[head], packed[k].at[head], out_sems.at[k, head])

    for k in range(2):
        for head in range(heads):
            arrival(2 * k, head).start()
            arrival(2 * k + 1, head).start()
    for k in range(2):
        for head in range(heads):
            arrival(2 * k, head).wait()
            arrival(2 * k + 1, head).wait()
            departure(k, head).start()
    for k in range(2):
        for head in range(heads):
            departure(k, head).wait()


def pack(arrays, heads):
    shapes = [(heads, a.shape[0], 2 * a.shape[1] // heads) for a in (arrays[0], arrays[2])]
    dtype = arrays[0].dtype
    return pl.pallas_call(
        pack_kernel,
        out_shape=[jax.ShapeDtypeStruct(shape, dtype) for shape in shapes],
        in_specs=[HBM] * 4,
        out_specs=[HBM] * 2,
        scratch_shapes=[
            *[pltpu.VMEM(shape, dtype) for shape in shapes],
            pltpu.SemaphoreType.DMA((4, heads)),
            pltpu.SemaphoreType.DMA((2, heads)),
        ],
        compiler_params=pltpu.CompilerParams(vmem_limit_bytes=60 << 20),
    )(*arrays)


def dot(a, b, contract):
    return lax.dot_general(a, b, ((contract[:1], contract[1:]), ((), ())), preferred_element_type=jnp.float32)


def fill(cat_ref, partners_ref, fars, kv_ref=None):
    blocks = cat_ref.shape[0]
    size = BLOCK_TOKENS
    for b in range(blocks):
        if kv_ref is not None:
            cat_ref[b, :size, :] = kv_ref[b * size : (b + 1) * size, :]
            if b:
                cat_ref[b, size : 2 * size, :] = kv_ref[(b - 1) * size : b * size, :]
        for j, far_ref in fars.items():
            if b == 0 and j == 0:
                cat_ref[b, size : 2 * size, :] = far_ref[(blocks - 1) * size :, :]
            pick = pl.multiple_of((partners_ref[b, 1 + j] & (blocks - 1)) * size, size)
            cat_ref[b, (2 + j) * size : (3 + j) * size, :] = far_ref[pl.ds(pick, size), :]


def early_kernel(partners_ref, kv_ref, *refs):
    fill(refs[-1], partners_ref, dict(zip(EARLY, refs[:-1], strict=True)), kv_ref)


def stack(qd_ref, b, first, heads):
    rows = slice(b * BLOCK_TOKENS, (b + 1) * BLOCK_TOKENS)
    columns = [slice((first + h) * HEAD_SIZE, (first + h + 1) * HEAD_SIZE) for h in range(heads)]
    return jnp.concatenate([qd_ref[rows, c] for c in columns], axis=0)


def gradients(probs_ref, dscores_ref, qd_ref, sums_ref, q_heads, b, low, high):
    rows = slice(low * BLOCK_TOKENS, high * BLOCK_TOKENS)
    query = stack(qd_ref, b, 0, q_heads)
    cotangent = stack(qd_ref, b, q_heads, q_heads)
    sums_ref[b, rows, :HEAD_SIZE] = SCALING * dot(dscores_ref[b, rows, :], query, (1, 0))
    sums_ref[b, rows, HEAD_SIZE:] = dot(probs_ref[b, rows, :], cotangent, (1, 0))


def main_kernel(far_count, q_heads, late, partners_ref, qd_ref, listed_ref, *refs):
    far_refs, refs = refs[: len(late)], refs[len(late) :]
    probs_ref, dscores_ref, cat_ref = refs[:3]
    part_refs = refs[3 : 3 + far_count]
    (sums_ref,) = refs[3 + far_count :]
    blocks = cat_ref.shape[0]
    slots = 2 + far_count
    size = BLOCK_TOKENS
    q_columns = q_heads * HEAD_SIZE
    pair = 2
    fill(cat_ref, partners_ref, dict(zip(late, far_refs, strict=True)))

    causal = lax.broadcasted_iota(jnp.int32, (size, size), 0) <= lax.broadcasted_iota(jnp.int32, (size, size), 1)
    causal = jnp.concatenate([causal] * pair, axis=1)
    for b in range(blocks):
        rows = slice(b * size, (b + 1) * size)
        keys = cat_ref[b, :, :HEAD_SIZE]
        values = cat_ref[b, :, HEAD_SIZE:]
        bias = [jnp.where(partners_ref[b, l] >= 0, 0.0, MASKED).astype(jnp.float32) for l in range(1 + far_count)]
        queries, cotangents = [], []
        for h in range(q_heads):
            queries.append(qd_ref[rows, h * HEAD_SIZE : (h + 1) * HEAD_SIZE])
            cotangents.append(qd_ref[rows, q_columns + h * HEAD_SIZE : q_columns + (h + 1) * HEAD_SIZE])
        for c in range(q_heads // pair):
            columns = slice(c * pair * size, (c + 1) * pair * size)
            query = jnp.concatenate(queries[c * pair : (c + 1) * pair], axis=0)
            cotangent = jnp.concatenate(cotangents[c * pair : (c + 1) * pair], axis=0)
            raw = dot(keys, query, (1, 1))
            scores = [jnp.where(causal, raw[:size], MASKED)]
            scores += [raw[(1 + l) * size : (2 + l) * size] + bias[l] for l in range(1 + far_count)]
            top = functools.reduce(jnp.maximum, scores)
            top = jnp.max(top, axis=0, keepdims=True)
            weights = [jnp.exp2((s - top) * (SCALING * math.log2(math.e))) for s in scores]
            total = jnp.sum(functools.reduce(jnp.add, weights), axis=0, keepdims=True)
            inverse = 1.0 / total
            dprobs = dot(values, cotangent, (1, 1))
            row_dot = jnp.zeros((size, pair * size), jnp.float32)
            for i in range(slots):
                weights[i] = weights[i] * inverse
                low = weights[i].astype(jnp.bfloat16)
                probs_ref[b, i * size : (i + 1) * size, columns] = low
                row_dot = row_dot + low.astype(jnp.float32) * dprobs[i * size : (i + 1) * size]
            row_dot = jnp.sum(row_dot, axis=0, keepdims=True)
            for i in range(slots):
                change = weights[i] * (dprobs[i * size : (i + 1) * size] - row_dot)
                dscores_ref[b, i * size : (i + 1) * size, columns] = change.astype(jnp.bfloat16)
        gradients(probs_ref, dscores_ref, qd_ref, sums_ref, q_heads, b, 2 if b else 1, slots)
    for j in range(far_count):
        at = slice((2 + j) * size, (3 + j) * size)
        for target in range(blocks):
            total = None
            for b in range(blocks):
                chosen = (partners_ref[b, 1 + j] & (blocks - 1)) == target
                term = jnp.where(chosen, sums_ref[b, at, :], 0.0)
                total = term if total is None else total + term
            if j == 0 and target == blocks - 1:
                total = total + sums_ref[0, size : 2 * size, :]
            part_refs[j][target * size : (target + 1) * size, :] = total.astype(jnp.bfloat16)


def outputs_kernel(q_heads, qd_ref, probs_ref, dscores_ref, cat_ref, attention_ref, grad_query_ref, own_ref, sums_ref):
    size = BLOCK_TOKENS
    blocks = probs_ref.shape[0]
    for b in range(blocks):
        rows = slice(b * size, (b + 1) * size)
        attention = dot(cat_ref[b, :, HEAD_SIZE:], probs_ref[b], (0, 0))
        grad_query = SCALING * dot(cat_ref[b, :, :HEAD_SIZE], dscores_ref[b], (0, 0))
        for h in range(q_heads):
            columns = slice(h * HEAD_SIZE, (h + 1) * HEAD_SIZE)
            at = slice(h * size, (h + 1) * size)
            attention_ref[rows, columns] = attention[:, at].T.astype(jnp.bfloat16)
            grad_query_ref[rows, columns] = grad_query[:, at].T.astype(jnp.bfloat16)
        gradients(probs_ref, dscores_ref, qd_ref, sums_ref, q_heads, b, 0, 2 if b else 1)
    for b in range(blocks):
        total = sums_ref[b, :size, :]
        if b + 1 < blocks:
            total = total + sums_ref[b + 1, size : 2 * size, :]
        own_ref[b * size : (b + 1) * size, :] = total


def sum_kernel(own_ref, *refs):
    key_ref, value_ref = refs[-2:]
    total = own_ref[...]
    for ref in refs[:-2]:
        total = total + ref[...].astype(jnp.float32)
    key_ref[...] = total[:, :HEAD_SIZE].astype(jnp.bfloat16)
    value_ref[...] = total[:, HEAD_SIZE:].astype(jnp.bfloat16)


def shards(query_projection, key_projection, value_projection, output_gradient, partners):
    heads = lax.axis_size("head")
    kv, qd = pack((key_projection, value_projection, query_projection, output_gradient), heads)
    kv = lax.all_to_all(kv, "head", 0, 0, tiled=True)
    qd = lax.all_to_all(qd, "head", 0, 0, tiled=True)
    kv = kv.reshape(-1, kv.shape[-1])
    qd = qd.reshape(-1, qd.shape[-1])
    tokens = kv.shape[0]
    blocks = tokens // BLOCK_TOKENS
    q_heads = qd.shape[1] // (2 * HEAD_SIZE)
    far_count = partners.shape[1] - 1
    fars = {j: (line if j in (4,) else ring)(kv, "seq", 2**j) for j in range(far_count) if j != 1}
    fars[1] = ring(fars[0], "seq", 1)
    late = (1, 4, 3)
    keys = (2 + far_count) * BLOCK_TOKENS
    big = (blocks, keys, q_heads * BLOCK_TOKENS)
    cat_type = jax.ShapeDtypeStruct((blocks, keys, 2 * HEAD_SIZE), jnp.bfloat16)
    listed = pl.pallas_call(
        early_kernel,
        out_shape=cat_type,
        in_specs=[SMEM] + [VMEM] * (1 + len(EARLY)),
        out_specs=VMEM,
        cost_estimate=pl.CostEstimate(flops=10**10, transcendentals=0, bytes_accessed=0),
        compiler_params=pltpu.CompilerParams(vmem_limit_bytes=8 << 20),
    )(partners, kv, *[fars[j] for j in EARLY])
    probs, dscores, cat, *parts = pl.pallas_call(
        functools.partial(main_kernel, far_count, q_heads, late),
        out_shape=[
            jax.ShapeDtypeStruct(big, jnp.bfloat16),
            jax.ShapeDtypeStruct(big, jnp.bfloat16),
            cat_type,
        ]
        + [jax.ShapeDtypeStruct((tokens, 2 * HEAD_SIZE), jnp.bfloat16)] * far_count,
        in_specs=[SMEM] + [VMEM] * (2 + len(late)),
        out_specs=[VMEM] * (3 + far_count),
        input_output_aliases={2: 2},
        scratch_shapes=[pltpu.VMEM((blocks, keys, 2 * HEAD_SIZE), jnp.float32)],
        compiler_params=pltpu.CompilerParams(vmem_limit_bytes=32 << 20),
    )(partners, qd, listed, *[fars[j] for j in late])
    received = [ring(part, "seq", -(2**j)) for j, part in enumerate(parts)]
    attention, grad_query, own = pl.pallas_call(
        functools.partial(outputs_kernel, q_heads),
        out_shape=[jax.ShapeDtypeStruct((tokens, q_heads * HEAD_SIZE), jnp.bfloat16)] * 2
        + [jax.ShapeDtypeStruct((tokens, 2 * HEAD_SIZE), jnp.float32)],
        in_specs=[VMEM] * 4,
        out_specs=[VMEM] * 3,
        scratch_shapes=[pltpu.VMEM((blocks, 2 * BLOCK_TOKENS, 2 * HEAD_SIZE), jnp.float32)],
        compiler_params=pltpu.CompilerParams(vmem_limit_bytes=32 << 20),
    )(qd, probs, dscores, cat)
    key_gradient, value_gradient = pl.pallas_call(
        sum_kernel,
        out_shape=[jax.ShapeDtypeStruct((tokens, HEAD_SIZE), jnp.bfloat16)] * 2,
        in_specs=[VMEM] * (1 + far_count),
        out_specs=[VMEM] * 2,
        compiler_params=pltpu.CompilerParams(vmem_limit_bytes=8 << 20),
    )(own, *received)
    return (attention, grad_query, key_gradient, value_gradient)


def solution(mesh):
    placed = (
        P(("seq", "head"), None),
        P(("seq", "head"), None),
        P(("seq", "head"), None),
        P(("seq", "head"), None),
        P("seq", None),
    )
    return jax.shard_map(
        shards,
        mesh=mesh,
        in_specs=placed,
        out_specs=(P("seq", "head"), P("seq", "head"), P("seq", "head"), P("seq", "head")),
        check_vma=False,
    )
```

```python
import functools
import math

import jax
import jax.numpy as jnp
from jax import lax
from jax.experimental import pallas as pl
from jax.experimental.pallas import tpu as pltpu
from jax.sharding import PartitionSpec as P

HEAD_SIZE = 128
BLOCK_TOKENS = 128
MASKED = -1e30
SCALING = 1.0 / math.sqrt(HEAD_SIZE)
VMEM = pl.BlockSpec(memory_space=pltpu.VMEM)
SMEM = pl.BlockSpec(memory_space=pltpu.SMEM)
HBM = pl.BlockSpec(memory_space=pltpu.HBM)
EARLY = (2, 0)


def ring(value, axis, steps):
    count = lax.axis_size(axis)
    return lax.ppermute(value, axis, [(s, (s + steps) % count) for s in range(count)])


def line(value, axis, steps):
    count = lax.axis_size(axis)
    pairs = [(s, s + steps) for s in range(count) if 0 <= s + steps < count]
    return lax.ppermute(value, axis, pairs)


def pack_kernel(*refs):
    sources, packed, held = refs[:4], refs[4:6], refs[6:8]
    in_sems, out_sems = refs[8:]
    heads = packed[0].shape[0]

    def arrival(i, head):
        width = sources[i].shape[1] // heads
        return pltpu.make_async_copy(
            sources[i].at[:, pl.ds(head * width, width)],
            held[i // 2].at[head, :, pl.ds((i % 2) * width, width)],
            in_sems.at[i, head],
        )

    def departure(k, head):
        return pltpu.make_async_copy(held[k].at[head], packed[k].at[head], out_sems.at[k, head])

    for k in range(2):
        for head in range(heads):
            arrival(2 * k, head).start()
            arrival(2 * k + 1, head).start()
    for k in range(2):
        for head in range(heads):
            arrival(2 * k, head).wait()
            arrival(2 * k + 1, head).wait()
            departure(k, head).start()
    for k in range(2):
        for head in range(heads):
            departure(k, head).wait()


def pack(arrays, heads):
    shapes = [(heads, a.shape[0], 2 * a.shape[1] // heads) for a in (arrays[0], arrays[2])]
    dtype = arrays[0].dtype
    return pl.pallas_call(
        pack_kernel,
        out_shape=[jax.ShapeDtypeStruct(shape, dtype) for shape in shapes],
        in_specs=[HBM] * 4,
        out_specs=[HBM] * 2,
        scratch_shapes=[
            *[pltpu.VMEM(shape, dtype) for shape in shapes],
            pltpu.SemaphoreType.DMA((4, heads)),
            pltpu.SemaphoreType.DMA((2, heads)),
        ],
        compiler_params=pltpu.CompilerParams(vmem_limit_bytes=60 << 20),
    )(*arrays)


def dot(a, b, contract):
    return lax.dot_general(a, b, ((contract[:1], contract[1:]), ((), ())), preferred_element_type=jnp.float32)


def fill(cat_ref, partners_ref, fars, kv_ref=None):
    blocks = cat_ref.shape[0]
    size = BLOCK_TOKENS
    for b in range(blocks):
        if kv_ref is not None:
            cat_ref[b, :size, :] = kv_ref[b * size : (b + 1) * size, :]
            if b:
                cat_ref[b, size : 2 * size, :] = kv_ref[(b - 1) * size : b * size, :]
        for j, far_ref in fars.items():
            if b == 0 and j == 0:
                cat_ref[b, size : 2 * size, :] = far_ref[(blocks - 1) * size :, :]
            pick = pl.multiple_of((partners_ref[b, 1 + j] & (blocks - 1)) * size, size)
            cat_ref[b, (2 + j) * size : (3 + j) * size, :] = far_ref[pl.ds(pick, size), :]


def early_kernel(partners_ref, kv_ref, *refs):
    fill(refs[-1], partners_ref, dict(zip(EARLY, refs[:-1], strict=True)), kv_ref)


def stack(qd_ref, b, first, heads):
    rows = slice(b * BLOCK_TOKENS, (b + 1) * BLOCK_TOKENS)
    columns = [slice((first + h) * HEAD_SIZE, (first + h + 1) * HEAD_SIZE) for h in range(heads)]
    return jnp.concatenate([qd_ref[rows, c] for c in columns], axis=0)


def gradients(probs_ref, dscores_ref, qd_ref, sums_ref, q_heads, b, low, high):
    rows = slice(low * BLOCK_TOKENS, high * BLOCK_TOKENS)
    query = stack(qd_ref, b, 0, q_heads)
    cotangent = stack(qd_ref, b, q_heads, q_heads)
    sums_ref[b, rows, :HEAD_SIZE] = SCALING * dot(dscores_ref[b, rows, :], query, (1, 0))
    sums_ref[b, rows, HEAD_SIZE:] = dot(probs_ref[b, rows, :], cotangent, (1, 0))


def main_kernel(far_count, q_heads, late, partners_ref, qd_ref, listed_ref, *refs):
    far_refs, refs = refs[: len(late)], refs[len(late) :]
    probs_ref, dscores_ref, cat_ref = refs[:3]
    part_refs = refs[3 : 3 + far_count]
    (sums_ref,) = refs[3 + far_count :]
    blocks = cat_ref.shape[0]
    slots = 2 + far_count
    size = BLOCK_TOKENS
    q_columns = q_heads * HEAD_SIZE
    pair = 4
    fill(cat_ref, partners_ref, dict(zip(late, far_refs, strict=True)))

    causal = lax.broadcasted_iota(jnp.int32, (size, size), 0) <= lax.broadcasted_iota(jnp.int32, (size, size), 1)
    causal = jnp.concatenate([causal] * pair, axis=1)
    for b in range(blocks):
        rows = slice(b * size, (b + 1) * size)
        keys = cat_ref[b, :, :HEAD_SIZE]
        values = cat_ref[b, :, HEAD_SIZE:]
        bias = [jnp.where(partners_ref[b, l] >= 0, 0.0, MASKED).astype(jnp.float32) for l in range(1 + far_count)]
        queries, cotangents = [], []
        for h in range(q_heads):
            queries.append(qd_ref[rows, h * HEAD_SIZE : (h + 1) * HEAD_SIZE])
            cotangents.append(qd_ref[rows, q_columns + h * HEAD_SIZE : q_columns + (h + 1) * HEAD_SIZE])
        for c in range(q_heads // pair):
            columns = slice(c * pair * size, (c + 1) * pair * size)
            query = jnp.concatenate(queries[c * pair : (c + 1) * pair], axis=0)
            cotangent = jnp.concatenate(cotangents[c * pair : (c + 1) * pair], axis=0)
            raw = dot(keys, query, (1, 1))
            scores = [jnp.where(causal, raw[:size], MASKED)]
            scores += [raw[(1 + l) * size : (2 + l) * size] + bias[l] for l in range(1 + far_count)]
            top = functools.reduce(jnp.maximum, scores)
            top = jnp.max(top, axis=0, keepdims=True)
            weights = [jnp.exp2((s - top) * (SCALING * math.log2(math.e))) for s in scores]
            total = jnp.sum(functools.reduce(jnp.add, weights), axis=0, keepdims=True)
            inverse = 1.0 / total
            dprobs = dot(values, cotangent, (1, 1))
            row_dot = jnp.zeros((size, pair * size), jnp.float32)
            for i in range(slots):
                weights[i] = weights[i] * inverse
                low = weights[i].astype(jnp.bfloat16)
                probs_ref[b, i * size : (i + 1) * size, columns] = low
                row_dot = row_dot + low.astype(jnp.float32) * dprobs[i * size : (i + 1) * size]
            row_dot = jnp.sum(row_dot, axis=0, keepdims=True)
            for i in range(slots):
                change = weights[i] * (dprobs[i * size : (i + 1) * size] - row_dot)
                dscores_ref[b, i * size : (i + 1) * size, columns] = change.astype(jnp.bfloat16)
        gradients(probs_ref, dscores_ref, qd_ref, sums_ref, q_heads, b, 2 if b else 1, slots)
    for j in range(far_count):
        at = slice((2 + j) * size, (3 + j) * size)
        for target in range(blocks):
            total = None
            for b in range(blocks):
                chosen = (partners_ref[b, 1 + j] & (blocks - 1)) == target
                term = jnp.where(chosen, sums_ref[b, at, :], 0.0)
                total = term if total is None else total + term
            if j == 0 and target == blocks - 1:
                total = total + sums_ref[0, size : 2 * size, :]
            part_refs[j][target * size : (target + 1) * size, :] = total.astype(jnp.bfloat16)


def outputs_kernel(q_heads, qd_ref, probs_ref, dscores_ref, cat_ref, attention_ref, grad_query_ref, own_ref, sums_ref):
    size = BLOCK_TOKENS
    blocks = probs_ref.shape[0]
    for b in range(blocks):
        rows = slice(b * size, (b + 1) * size)
        attention = dot(cat_ref[b, :, HEAD_SIZE:], probs_ref[b], (0, 0))
        grad_query = SCALING * dot(cat_ref[b, :, :HEAD_SIZE], dscores_ref[b], (0, 0))
        for h in range(q_heads):
            columns = slice(h * HEAD_SIZE, (h + 1) * HEAD_SIZE)
            at = slice(h * size, (h + 1) * size)
            attention_ref[rows, columns] = attention[:, at].T.astype(jnp.bfloat16)
            grad_query_ref[rows, columns] = grad_query[:, at].T.astype(jnp.bfloat16)
        gradients(probs_ref, dscores_ref, qd_ref, sums_ref, q_heads, b, 0, 2 if b else 1)
    for b in range(blocks):
        total = sums_ref[b, :size, :]
        if b + 1 < blocks:
            total = total + sums_ref[b + 1, size : 2 * size, :]
        own_ref[b * size : (b + 1) * size, :] = total


def sum_kernel(own_ref, *refs):
    key_ref, value_ref = refs[-2:]
    total = own_ref[...]
    for ref in refs[:-2]:
        total = total + ref[...].astype(jnp.float32)
    key_ref[...] = total[:, :HEAD_SIZE].astype(jnp.bfloat16)
    value_ref[...] = total[:, HEAD_SIZE:].astype(jnp.bfloat16)


def shards(query_projection, key_projection, value_projection, output_gradient, partners):
    heads = lax.axis_size("head")
    kv, qd = pack((key_projection, value_projection, query_projection, output_gradient), heads)
    kv = lax.all_to_all(kv, "head", 0, 0, tiled=True)
    qd = lax.all_to_all(qd, "head", 0, 0, tiled=True)
    kv = kv.reshape(-1, kv.shape[-1])
    qd = qd.reshape(-1, qd.shape[-1])
    tokens = kv.shape[0]
    blocks = tokens // BLOCK_TOKENS
    q_heads = qd.shape[1] // (2 * HEAD_SIZE)
    far_count = partners.shape[1] - 1
    fars = {j: (line if j in (4,) else ring)(kv, "seq", 2**j) for j in range(far_count) if j != 1}
    fars[1] = ring(fars[0], "seq", 1)
    late = (4, 3, 1)
    keys = (2 + far_count) * BLOCK_TOKENS
    big = (blocks, keys, q_heads * BLOCK_TOKENS)
    cat_type = jax.ShapeDtypeStruct((blocks, keys, 2 * HEAD_SIZE), jnp.bfloat16)
    listed = pl.pallas_call(
        early_kernel,
        out_shape=cat_type,
        in_specs=[SMEM] + [VMEM] * (1 + len(EARLY)),
        out_specs=VMEM,
        cost_estimate=pl.CostEstimate(flops=10**10, transcendentals=0, bytes_accessed=0),
        compiler_params=pltpu.CompilerParams(vmem_limit_bytes=8 << 20),
    )(partners, kv, *[fars[j] for j in EARLY])
    probs, dscores, cat, *parts = pl.pallas_call(
        functools.partial(main_kernel, far_count, q_heads, late),
        out_shape=[
            jax.ShapeDtypeStruct(big, jnp.bfloat16),
            jax.ShapeDtypeStruct(big, jnp.bfloat16),
            cat_type,
        ]
        + [jax.ShapeDtypeStruct((tokens, 2 * HEAD_SIZE), jnp.bfloat16)] * far_count,
        in_specs=[SMEM] + [VMEM] * (2 + len(late)),
        out_specs=[VMEM] * (3 + far_count),
        input_output_aliases={2: 2},
        scratch_shapes=[pltpu.VMEM((blocks, keys, 2 * HEAD_SIZE), jnp.float32)],
        compiler_params=pltpu.CompilerParams(vmem_limit_bytes=32 << 20),
    )(partners, qd, listed, *[fars[j] for j in late])
    received = [ring(part, "seq", -(2**j)) for j, part in enumerate(parts)]
    attention, grad_query, own = pl.pallas_call(
        functools.partial(outputs_kernel, q_heads),
        out_shape=[jax.ShapeDtypeStruct((tokens, q_heads * HEAD_SIZE), jnp.bfloat16)] * 2
        + [jax.ShapeDtypeStruct((tokens, 2 * HEAD_SIZE), jnp.float32)],
        in_specs=[VMEM] * 4,
        out_specs=[VMEM] * 3,
        scratch_shapes=[pltpu.VMEM((blocks, 2 * BLOCK_TOKENS, 2 * HEAD_SIZE), jnp.float32)],
        compiler_params=pltpu.CompilerParams(vmem_limit_bytes=32 << 20),
    )(qd, probs, dscores, cat)
    key_gradient, value_gradient = pl.pallas_call(
        sum_kernel,
        out_shape=[jax.ShapeDtypeStruct((tokens, HEAD_SIZE), jnp.bfloat16)] * 2,
        in_specs=[VMEM] * (1 + far_count),
        out_specs=[VMEM] * 2,
        compiler_params=pltpu.CompilerParams(vmem_limit_bytes=8 << 20),
    )(own, *received)
    return (attention, grad_query, key_gradient, value_gradient)


def solution(mesh):
    placed = (
        P(("seq", "head"), None),
        P(("seq", "head"), None),
        P(("seq", "head"), None),
        P(("seq", "head"), None),
        P("seq", None),
    )
    return jax.shard_map(
        shards,
        mesh=mesh,
        in_specs=placed,
        out_specs=(P("seq", "head"), P("seq", "head"), P("seq", "head"), P("seq", "head")),
        check_vma=False,
    )
```
